1024 devices in a mesh: inst: 16 (over z_lo, x), dom: 64 (over y, z_hi, core).
Axes of the slice: x: 4, y: 8, z: 16 (z_hi: 4, z_lo: 4; z = z_hi * 4 + z_lo), core: 2. Of those that a mesh axis runs over, the one named last changes fastest.
Arguments:
- perturbation: float32 [16, 6, 1024, 1024], P('inst', None, 'dom'), may hold values from -6 to 6
- jacobian: float32 [16, 6, 6, 1024, 1024], P('inst', None, None, 'dom'), may hold values from -2.5 to 2.5
- flux_theta: float32 [6, 6], replicated, may hold values from -2.5 to 2.5
- flux_merid: float32 [6, 6], replicated, may hold values from -2.5 to 2.5
- donor_rows: int32 [16, 2, 1024], P('inst', None, 'dom'), may hold values from 0 to 1023
- donor_weights: float32 [16, 2, 1024], P('inst', None, 'dom'), may hold values from 0 to 1
Outputs:
- product: float32 [16, 6, 1024, 1024], P('inst', None, 'dom')
The draws below stay inside these ranges and needn't reach their ends.
Inputs may be any that keep to these rules, and one draw needn't show every extreme that they name: `donor_rows`: donor lines are global circumferential indices on the outlet face.
All inputs are finite; a program needn't handle non-finite values.
Results may differ from the reference program's by a relative error of at most 0.0014.
The reference program's roundings to bfloat16 on the way (of `low`) count: a program that leaves them out, or rounds other values in their place, can miss the bound.
Values may be sent and summed in bfloat16 or wider, within the bound.
No kernel may reach another device: no remote copies, remote signals or barrier semaphores. Data moves between devices by JAX's collectives and lax.ppermute only.
A program may use at most 32 MiB of HBM per device.

```python
import jax
import jax.numpy as jnp
from jax import lax

VARS = 6
NM = 1024
INSTANCES = 16
NTHETA = 1024


def set_ends(values, stream_key, smallest, top_value):
    longest = values.shape.index(max(values.shape))
    spots = []
    for shift in (0, 1):
        where = [jax.random.randint(jax.random.fold_in(stream_key, axis), (), 0, length) for axis, length in enumerate(values.shape)]
        where[longest] = (where[longest] + shift) % values.shape[longest]
        spots.append(tuple(where))
    return values.at[spots[0]].set(smallest).at[spots[1]].set(top_value)


def block_levels(own_key, extent, cuts, low, top_value):
    factor_of, own = 1.0, jax.random.fold_in(own_key, 6)
    for axis_at, parts in cuts:
        steps = jnp.exp(jax.random.uniform(jax.random.fold_in(own, axis_at), (parts,), jnp.float32, low / len(cuts), top_value / len(cuts)))
        factor_of = factor_of * jnp.repeat(steps, extent[axis_at] // parts).reshape([-1 if axis == axis_at else 1 for axis in range(len(extent))])
    return factor_of


def bell_draw(own_key, dims, scale, bound, cuts=(), kind=jnp.bfloat16):
    values = jax.random.normal(own_key, dims, jnp.float32) * scale
    if len(cuts) > 0:
        values = block_levels(own_key, dims, cuts, -0.22, 0.18) * values
    return jnp.clip(values, min=-bound, max=bound).astype(kind)


def setup_inputs(seed: int = 0) -> dict:
    key_of = jax.random.split(jax.random.key(seed), 7)
    return {
        "perturbation": bell_draw(key_of[0], (INSTANCES, VARS, NTHETA, NM), 1.0, 6.0, ((0, 16), (2, 64)), jnp.float32),
        "jacobian": bell_draw(key_of[1], (INSTANCES, VARS, VARS, NTHETA, NM), VARS ** -0.5, 2.5, ((0, 16), (3, 64)), jnp.float32),
        "flux_theta": bell_draw(key_of[2], (VARS, VARS), VARS ** -0.5, 2.5, (), jnp.float32),
        "flux_merid": bell_draw(key_of[3], (VARS, VARS), VARS ** -0.5, 2.5, (), jnp.float32),
        "donor_rows": set_ends(jax.random.randint(key_of[4], (INSTANCES, 2, NTHETA), 0, NTHETA), jax.random.fold_in(key_of[4], 1), 0, NTHETA - 1).astype(jnp.int32),
        "donor_weights": jnp.clip(1.0 * jax.random.uniform(key_of[5], (INSTANCES, 2, NTHETA), jnp.float32) ** block_levels(key_of[5], (INSTANCES, 2, NTHETA), ((0, 16), (2, 64)), -0.2, 0.2), 0.0, 1.0),
    }


OMEGA = 0.5
NYQUIST = 2.0


def spectral_row(count):
    offs = jnp.arange(count, dtype=jnp.int32)
    sign = (1 - 2 * (offs % 2)).astype(jnp.float32)
    safe = jnp.maximum(offs, 1).astype(jnp.float32)
    angle = jnp.pi * safe / count
    cotan = jnp.where(offs == 0, 0.0, jnp.cos(angle) / jnp.sin(angle)).astype(jnp.float32)
    return (OMEGA * 0.5 * sign * cotan + NYQUIST * sign / count).astype(jnp.float32)


def reference(perturbation, jacobian, flux_theta, flux_merid, donor_rows, donor_weights):
    count = INSTANCES
    row = spectral_row(count)
    idx = jnp.arange(count, dtype=jnp.int32)
    matrix = row[(idx[:, None] - idx[None, :]) % count]
    low = perturbation.astype(jnp.bfloat16).astype(jnp.float32)
    temporal = jnp.einsum("ij,jvtm->ivtm", matrix, low, precision=lax.Precision.HIGHEST)
    temporal = temporal + matrix[0, 0] * (perturbation - low)
    dtheta = jnp.roll(perturbation, -1, axis=2) - jnp.roll(perturbation, 1, axis=2)
    padded = jnp.pad(perturbation, ((0, 0), (0, 0), (0, 0), (1, 1)))
    dmerid = padded[:, :, :, 2:] - padded[:, :, :, :-2]
    spatial = jnp.einsum("iabtm,ibtm->iatm", jacobian, perturbation, precision=lax.Precision.HIGHEST)
    spatial = spatial + jnp.einsum("ab,ibtm->iatm", flux_theta, dtheta, precision=lax.Precision.HIGHEST)
    spatial = spatial + jnp.einsum("ab,ibtm->iatm", flux_merid, dmerid, precision=lax.Precision.HIGHEST)
    outlet = perturbation[:, :, :, NM - 1]
    interp = jnp.zeros_like(outlet)
    for donor in range(2):
        picked = jnp.take_along_axis(outlet, jnp.broadcast_to(donor_rows[:, donor][:, None, :], outlet.shape).astype(jnp.int32), axis=2)
        interp = interp + donor_weights[:, donor][:, None, :] * picked
    interface = perturbation[:, :, :, 0] - interp
    product = temporal + spatial
    return product.at[:, :, :, 0].add(interface)
```

```python
import jax
import jax.numpy as jnp
import numpy as np
from jax import lax
from jax.sharding import Mesh, PartitionSpec as P

OMEGA = 0.5
NYQUIST = 2.0
INST = "inst"
DOM = ("ring", "far", "core")


def spectral_row(count):
    offs = jnp.arange(count, dtype=jnp.int32)
    sign = (1 - 2 * (offs % 2)).astype(jnp.float32)
    safe = jnp.maximum(offs, 1).astype(jnp.float32)
    angle = jnp.pi * safe / count
    cotan = jnp.where(offs == 0, 0.0, jnp.cos(angle) / jnp.sin(angle))
    return OMEGA * 0.5 * sign * cotan + NYQUIST * sign / count


def told_to_all(value, axis):
    count = lax.axis_size(axis)
    copies = jnp.broadcast_to(value[None], (count,) + value.shape)
    return lax.all_to_all(copies, axis, 0, 0, tiled=True)


def shards(perturbation, jacobian, flux_theta, flux_merid, donor_rows, donor_weights):
    count = lax.axis_size(INST)
    table = spectral_row(count)
    own = perturbation[0]
    nvar, rows, cells = own.shape
    lanes = cells // 8
    low = own.astype(jnp.bfloat16)
    blocks = low.reshape(2, nvar // 2, rows, 8, lanes).transpose(0, 3, 1, 2, 4)
    blocks = blocks.reshape(count, nvar // 2, rows, lanes)
    gathered = lax.all_to_all(blocks, INST, 0, 0, tiled=True)
    idx = jnp.arange(count, dtype=jnp.int32)
    matrix = table[(idx[:, None] - idx[None, :]) % count]
    mixed = jnp.einsum(
        "ij,jvtm->ivtm", matrix, gathered.astype(jnp.float32), precision=lax.Precision.HIGHEST
    )
    back = lax.all_to_all(mixed, INST, 0, 0, tiled=True)
    back = back.reshape(2, 8, nvar // 2, rows, lanes).transpose(0, 2, 3, 1, 4)
    temporal = back.reshape(nvar, rows, cells)
    temporal = temporal + table[0] * (own - low.astype(jnp.float32))

    ndom = lax.axis_size(DOM)
    before = lax.ppermute(own[:, -1:], DOM, [(i, (i + 1) % ndom) for i in range(ndom)])
    after = lax.ppermute(own[:, :1], DOM, [((i + 1) % ndom, i) for i in range(ndom)])
    padded = jnp.concatenate([before, own, after], axis=1)
    dtheta = padded[:, 2:] - padded[:, :-2]
    merid_pad = jnp.pad(own, ((0, 0), (0, 0), (1, 1)))
    dmerid = merid_pad[:, :, 2:] - merid_pad[:, :, :-2]
    spatial = jnp.sum(jacobian[0] * own[None], axis=1)
    for b in range(nvar):
        spatial = spatial + flux_theta[:, b, None, None] * dtheta[b][None]
        spatial = spatial + flux_merid[:, b, None, None] * dmerid[b][None]

    face = own[:, :, cells - 1]
    face = lax.all_gather(face, "core", axis=0)
    face = told_to_all(face, "far")
    face = told_to_all(face, "ring")
    outlet = face.transpose(3, 0, 1, 2, 4).reshape(nvar, ndom * rows)
    interp = jnp.zeros((nvar, rows), jnp.float32)
    for donor in range(2):
        picked = jnp.take(outlet, donor_rows[0, donor], axis=1)
        interp = interp + donor_weights[0, donor][None, :] * picked
    interface = own[:, :, 0] - interp
    product = temporal + spatial
    return product.at[:, :, 0].add(interface)[None]


def solution(mesh):
    inst = mesh.devices.shape[0]
    fine = Mesh(mesh.devices.reshape(inst, 8, 4, 2), (INST,) + DOM)
    in_specs = (
        P(INST, None, DOM, None),
        P(INST, None, None, DOM, None),
        P(),
        P(),
        P(INST, None, DOM),
        P(INST, None, DOM),
    )
    out_specs = P(INST, None, DOM, None)
    return jax.shard_map(shards, mesh=fine, in_specs=in_specs, out_specs=out_specs, check_vma=False)
```

```python
import functools
import math

import jax
import jax.numpy as jnp
from jax import lax
from jax.experimental import pallas as pl
from jax.experimental.pallas import tpu as pltpu
from jax.sharding import Mesh, PartitionSpec as P

OMEGA = 0.5
NYQUIST = 2.0
INST = "inst"
RING, FAR, CORE = "ring", "far", "core"
DOM = (RING, FAR, CORE)
LANES = 128
F32 = jnp.float32
VMEM_BYTES = 12 * 2**20


def whole(count):
    return [pl.BlockSpec(memory_space=pltpu.VMEM) for _ in range(count)]


def call(body, operands, specs, outs, flops, name, scratch=()):
    moved = sum(math.prod(v.shape) * v.dtype.itemsize for v in list(operands) + list(outs))
    return pl.pallas_call(
        body,
        out_shape=outs,
        in_specs=specs,
        out_specs=whole(len(outs)),
        scratch_shapes=scratch,
        compiler_params=pltpu.CompilerParams(vmem_limit_bytes=VMEM_BYTES),
        cost_estimate=pl.CostEstimate(flops=flops, bytes_accessed=moved, transcendentals=0),
        name=name,
    )(*operands)


def antisymmetric(count):
    return [OMEGA * 0.5 * (-1) ** k / math.tan(math.pi * k / count) for k in range(1, count // 2)]


def prepare(p_ref, blocks_ref, face_ref, sibling_ref, outer_ref):
    nvar, rows, cells = p_ref.shape[1:]
    chunks = cells // LANES
    upper = lax.axis_index(CORE) == 1
    low = p_ref[0].astype(jnp.bfloat16)
    third = nvar // 2
    for h in range(2):
        for c in range(chunks):
            blocks_ref[h * chunks + c] = low[h * third : (h + 1) * third, :, c * LANES : (c + 1) * LANES]
    lane = lax.broadcasted_iota(jnp.int32, (rows, LANES), 1)
    line = lax.broadcasted_iota(jnp.int32, (rows, LANES), 0)
    picked = jnp.zeros((rows, LANES), F32)
    for v in range(nvar):
        last = jnp.broadcast_to(p_ref[0, v, :, cells - 1 : cells], (rows, LANES))
        picked = jnp.where(lane == v * rows + line, last, picked)
    face = jnp.sum(picked, axis=0, keepdims=True)
    face_ref[...] = jnp.broadcast_to(face[None], face_ref.shape)
    first, final = p_ref[0, :, 0, :], p_ref[0, :, rows - 1, :]
    sibling_ref[...] = jnp.where(upper, first, final)
    outer_ref[...] = jnp.where(upper, final, first)


def mix(got_ref, near_ref, mixed_ref, told_ref):
    count, third = got_ref.shape[0], got_ref.shape[1]
    half = count // 2
    deriv = antisymmetric(count)
    for v in range(third):
        a = [got_ref[j, v].astype(F32) for j in range(count)]
        even, odd = a[0], a[1]
        for j in range(2, count, 2):
            even, odd = even + a[j], odd + a[j + 1]
        filt = (even - odd) * (NYQUIST / count)
        for i in range(half):
            gap = [a[(i - k) % count] - a[(i + k) % count] for k in range(1, half)]
            here, there = deriv[0] * gap[0], deriv[half - 2] * gap[0]
            for k in range(1, half - 1):
                here, there = here + deriv[k] * gap[k], there + deriv[half - 2 - k] * gap[k]
            sign = filt if i % 2 == 0 else -filt
            mixed_ref[i, v] = here + sign
            mixed_ref[i + half, v] = (sign if half % 2 == 0 else -sign) - there
    told_ref[...] = jnp.broadcast_to(near_ref[:, 0, :][None], told_ref.shape)


def space(count, p_ref, jac_ref, theta_ref, merid_ref, pair_ref, outer_ref, out_ref, dm_ref):
    nvar, rows, cells = p_ref.shape[1:]
    core = lax.axis_index(CORE)
    upper = core == 1
    lane = lax.broadcasted_iota(jnp.int32, (rows, cells), 1)
    line = lax.broadcasted_iota(jnp.int32, (rows, LANES), 0)
    for b in range(nvar):
        x = p_ref[0, b]
        right = jnp.where(lane == cells - 1, 0.0, pltpu.roll(x, cells - 1, 1))
        left = jnp.where(lane == 0, 0.0, pltpu.roll(x, 1, 1))
        dm_ref[b] = right - left
    for c in range(cells // LANES):
        part = slice(c * LANES, (c + 1) * LANES)
        sibling = pair_ref[1 - core, :, part]
        outer = outer_ref[:, part]
        before = jnp.where(upper, sibling, outer)
        after = jnp.where(upper, outer, sibling)
        xs, ths, dms = [], [], []
        for b in range(nvar):
            x = p_ref[0, b, :, part]
            up = jnp.where(line == rows - 1, after[b : b + 1], pltpu.roll(x, rows - 1, 0))
            down = jnp.where(line == 0, before[b : b + 1], pltpu.roll(x, 1, 0))
            xs.append(x)
            ths.append(up - down)
            dms.append(dm_ref[b, :, part])
        for a in range(nvar):
            acc = (xs[a] - xs[a].astype(jnp.bfloat16).astype(F32)) * (NYQUIST / count)
            for b in range(nvar):
                acc = acc + jac_ref[0, a, b, :, part] * xs[b]
                acc = acc + theta_ref[a, b] * ths[b]
                acc = acc + merid_ref[a, b] * dms[b]
            out_ref[a, :, part] = acc


def finish(sum_ref, back_ref, faces_ref, p_ref, weights_ref, rows_ref, out_ref, got_ref):
    nvar, rows, cells = sum_ref.shape
    chunks = cells // LANES
    third = nvar // 2
    for h in range(2):
        for c in range(chunks):
            part = slice(c * LANES, (c + 1) * LANES)
            own = slice(h * third, (h + 1) * third)
            out_ref[0, own, :, part] = sum_ref[own, :, part] + back_ref[h * chunks + c]
    lane = lax.broadcasted_iota(jnp.int32, (rows, LANES), 1)
    line = lax.broadcasted_iota(jnp.int32, (rows, LANES), 0)
    total = jnp.zeros((rows, LANES), F32)
    for donor in range(2):
        within = jnp.zeros((rows, LANES), jnp.int32)
        for t in range(rows):
            r = rows_ref[0, donor, t]
            device, spot = r // rows, r % rows
            got_ref[donor, t : t + 1, :] = faces_ref[device // 8, pl.ds(device % 8, 1), :]
            within = jnp.where(line == t, spot, within)
        weight = jnp.broadcast_to(weights_ref[0, donor : donor + 1, :], (rows, rows))
        square = (rows, rows)
        eye = lax.broadcasted_iota(jnp.int32, square, 0) == lax.broadcasted_iota(jnp.int32, square, 1)
        weight = jnp.sum(jnp.where(eye, weight, 0.0), axis=1, keepdims=True)
        total = total + jnp.where(lane % rows == within, got_ref[donor], 0.0) * weight
    for v in range(nvar):
        mine = jnp.where(lane // rows == v, total, 0.0)
        interp = jnp.sum(mine, axis=1, keepdims=True)
        head = out_ref[0, v, :, :LANES]
        interface = p_ref[0, v, :, :LANES] - interp
        out_ref[0, v, :, :LANES] = head + jnp.where(lane == 0, interface, 0.0)


def shards(perturbation, jacobian, flux_theta, flux_merid, donor_rows, donor_weights):
    count, far, ring = lax.axis_size(INST), lax.axis_size(FAR), lax.axis_size(RING)
    ndom = lax.axis_size(DOM)
    _, nvar, rows, cells = perturbation.shape
    smem = pl.BlockSpec(memory_space=pltpu.SMEM)
    blocks, face, sibling, outer = call(
        prepare,
        (perturbation,),
        whole(1),
        (
            jax.ShapeDtypeStruct((count, nvar // 2, rows, LANES), jnp.bfloat16),
            jax.ShapeDtypeStruct((far * 2, 8, LANES), F32),
            jax.ShapeDtypeStruct((nvar, cells), F32),
            jax.ShapeDtypeStruct((nvar, cells), F32),
        ),
        10**6,
        "prepare",
    )
    swaps = [(c, (c + (1 if c % 2 else -1)) % ndom) for c in range(ndom)]
    outer = lax.ppermute(outer, DOM, swaps)
    near = lax.all_to_all(face, (FAR, CORE), 0, 0, tiled=True)
    got = lax.all_to_all(blocks, INST, 0, 0, tiled=True)
    pair = lax.all_gather(sibling, CORE, axis=0)
    total = call(
        functools.partial(space, count),
        (perturbation, jacobian, flux_theta, flux_merid, pair, outer),
        whole(2) + [smem, smem] + whole(2),
        (jax.ShapeDtypeStruct((nvar, rows, cells), F32),),
        2 * 18 * nvar * rows * cells,
        "space",
        [pltpu.VMEM((nvar, rows, cells), F32)],
    )[0]
    mixed, told = call(
        mix,
        (got, near),
        whole(2),
        (
            jax.ShapeDtypeStruct((count, nvar // 2, rows, LANES), F32),
            jax.ShapeDtypeStruct((ring, far * 2, LANES), F32),
        ),
        2 * 16 * nvar * rows * cells,
        "mix",
    )
    back = lax.all_to_all(mixed, INST, 0, 0, tiled=True)
    faces = lax.all_to_all(told, RING, 0, 0, tiled=True)
    return call(
        finish,
        (total, back, faces, perturbation, donor_weights, donor_rows),
        whole(5) + [smem],
        (jax.ShapeDtypeStruct(perturbation.shape, F32),),
        3 * nvar * rows * cells,
        "finish",
        [pltpu.VMEM((2, rows, LANES), F32)],
    )[0]


def solution(mesh):
    inst = mesh.devices.shape[0]
    fine = Mesh(mesh.devices.reshape(inst, 8, 4, 2), (INST,) + DOM)
    in_specs = (
        P(INST, None, DOM, None),
        P(INST, None, None, DOM, None),
        P(),
        P(),
        P(INST, None, DOM),
        P(INST, None, DOM),
    )
    out_specs = P(INST, None, DOM, None)
    return jax.shard_map(shards, mesh=fine, in_specs=in_specs, out_specs=out_specs, check_vma=False)
```

```python
import functools
import math

import jax
import jax.numpy as jnp
from jax import lax
from jax.experimental import pallas as pl
from jax.experimental.pallas import tpu as pltpu
from jax.sharding import Mesh, PartitionSpec as P

OMEGA = 0.5
NYQUIST = 2.0
INST = "inst"
RING, FAR, CORE = "ring", "far", "core"
DOM = (RING, FAR, CORE)
LANES = 128
F32 = jnp.float32
VMEM_BYTES = 12 * 2**20


def whole(count):
    return [pl.BlockSpec(memory_space=pltpu.VMEM) for _ in range(count)]


def call(body, operands, specs, outs, flops, name, scratch=()):
    moved = sum(math.prod(v.shape) * v.dtype.itemsize for v in list(operands) + list(outs))
    return pl.pallas_call(
        body,
        out_shape=outs,
        in_specs=specs,
        out_specs=whole(len(outs)),
        scratch_shapes=scratch,
        compiler_params=pltpu.CompilerParams(vmem_limit_bytes=VMEM_BYTES),
        cost_estimate=pl.CostEstimate(flops=flops, bytes_accessed=moved, transcendentals=0),
        name=name,
    )(*operands)


def antisymmetric(count):
    return [OMEGA * 0.5 * (-1) ** k / math.tan(math.pi * k / count) for k in range(1, count // 2)]


def prepare(p_ref, blocks_ref, face_ref, sibling_ref, outer_ref):
    nvar, rows, cells = p_ref.shape[1:]
    chunks = cells // LANES
    upper = lax.axis_index(CORE) == 1
    low = p_ref[0].astype(jnp.bfloat16)
    third = nvar // 2
    for h in range(2):
        for c in range(chunks):
            blocks_ref[h * chunks + c] = low[h * third : (h + 1) * third, :, c * LANES : (c + 1) * LANES]
    lane = lax.broadcasted_iota(jnp.int32, (rows, LANES), 1)
    line = lax.broadcasted_iota(jnp.int32, (rows, LANES), 0)
    picked = jnp.zeros((rows, LANES), F32)
    for v in range(nvar):
        last = jnp.broadcast_to(p_ref[0, v, :, cells - 1 : cells], (rows, LANES))
        picked = jnp.where(lane == v * rows + line, last, picked)
    face = jnp.sum(picked, axis=0, keepdims=True)
    for k in range(face_ref.shape[0]):
        face_ref[k] = face
    first, final = p_ref[0, :, 0, :], p_ref[0, :, rows - 1, :]
    sibling_ref[...] = jnp.where(upper, first, final)
    outer_ref[...] = jnp.where(upper, final, first)


def mix(got_ref, outer_ref, pair_ref, mixed_ref):
    del outer_ref, pair_ref
    count, third = got_ref.shape[0], got_ref.shape[1]
    half = count // 2
    deriv = antisymmetric(count)
    for v in range(third):
        a = [got_ref[j, v].astype(F32) for j in range(count)]
        even, odd = a[0], a[1]
        for j in range(2, count, 2):
            even, odd = even + a[j], odd + a[j + 1]
        filt = (even - odd) * (NYQUIST / count)
        for i in range(half):
            gap = [a[(i - k) % count] - a[(i + k) % count] for k in range(1, half)]
            here, there = deriv[0] * gap[0], deriv[half - 2] * gap[0]
            for k in range(1, half - 1):
                here, there = here + deriv[k] * gap[k], there + deriv[half - 2 - k] * gap[k]
            sign = filt if i % 2 == 0 else -filt
            mixed_ref[i, v] = here + sign
            mixed_ref[i + half, v] = (sign if half % 2 == 0 else -sign) - there


def space(count, p_hbm, jac_hbm, theta_hbm, merid_hbm, pair_ref, outer_ref, out_ref, p_ref, jac_ref, theta_ref, merid_ref, dm_ref, sems):
    copies = [
        pltpu.make_async_copy(source, target, sems.at[k])
        for k, (source, target) in enumerate(
            [(p_hbm, p_ref), (theta_hbm, theta_ref), (merid_hbm, merid_ref), (jac_hbm, jac_ref)]
        )
    ]
    for copy in copies:
        copy.start()
    nvar, rows, cells = p_ref.shape[1:]
    core = lax.axis_index(CORE)
    upper = core == 1
    lane = lax.broadcasted_iota(jnp.int32, (rows, cells), 1)
    line = lax.broadcasted_iota(jnp.int32, (rows, LANES), 0)
    narrow = lax.broadcasted_iota(jnp.int32, (rows, LANES), 1)
    copies[0].wait()
    for b in range(nvar):
        x = p_ref[0, b]
        right = jnp.where(lane == cells - 1, 0.0, pltpu.roll(x, cells - 1, 1))
        left = jnp.where(lane == 0, 0.0, pltpu.roll(x, 1, 1))
        dm_ref[b] = right - left
    for copy in copies[1:]:
        copy.wait()
    for c in range(cells // LANES):
        part = slice(c * LANES, (c + 1) * LANES)
        sibling = pair_ref[1 - core, :, part]
        outer = outer_ref[:, part]
        before = jnp.where(upper, sibling, outer)
        after = jnp.where(upper, outer, sibling)
        xs, ths, dms = [], [], []
        for b in range(nvar):
            x = p_ref[0, b, :, part]
            up = jnp.where(line == rows - 1, after[b : b + 1], pltpu.roll(x, rows - 1, 0))
            down = jnp.where(line == 0, before[b : b + 1], pltpu.roll(x, 1, 0))
            xs.append(x)
            ths.append(up - down)
            dms.append(dm_ref[b, :, part])
        for a in range(nvar):
            acc = (xs[a] - xs[a].astype(jnp.bfloat16).astype(F32)) * (NYQUIST / count)
            if c == 0:
                acc = acc + jnp.where(narrow == 0, xs[a], 0.0)
            for b in range(nvar):
                acc = acc + jac_ref[0, a, b, :, part] * xs[b]
                acc = acc + theta_ref[a, b] * ths[b]
                acc = acc + merid_ref[a, b] * dms[b]
            out_ref[a, :, part] = acc


def finish(sum_ref, back_ref, f0_ref, f1_ref, f2_ref, f3_ref, weights_ref, rows_ref, out_ref, faces_ref, got_ref):
    nvar, rows, cells = sum_ref.shape
    chunks = cells // LANES
    third = nvar // 2
    near = f0_ref.shape[0]
    for s, ref in enumerate((f0_ref, f1_ref, f2_ref, f3_ref)):
        for k in range(near):
            faces_ref[s * near + k] = ref[k]
    me = lax.axis_index(FAR)
    for h in range(2):
        for c in range(chunks):
            part = slice(c * LANES, (c + 1) * LANES)
            own = slice(h * third, (h + 1) * third)
            out_ref[0, own, :, part] = sum_ref[own, :, part] + back_ref[h * chunks + c]
    lane = lax.broadcasted_iota(jnp.int32, (rows, LANES), 1)
    line = lax.broadcasted_iota(jnp.int32, (rows, LANES), 0)
    total = jnp.zeros((rows, LANES), F32)
    for donor in range(2):
        within = jnp.zeros((rows, LANES), jnp.int32)
        for t in range(rows):
            r = rows_ref[0, donor, t]
            device, spot = r // rows, r % rows
            back = (me + 4 - (device // 2) % 4) % 4
            got_ref[donor, t : t + 1, :] = faces_ref[back * near + device // 8 * 2 + device % 2]
            within = jnp.where(line == t, spot, within)
        weight = jnp.broadcast_to(weights_ref[0, donor : donor + 1, :], (rows, rows))
        square = (rows, rows)
        eye = lax.broadcasted_iota(jnp.int32, square, 0) == lax.broadcasted_iota(jnp.int32, square, 1)
        weight = jnp.sum(jnp.where(eye, weight, 0.0), axis=1, keepdims=True)
        total = total + jnp.where(lane % rows == within, got_ref[donor], 0.0) * weight
    for v in range(nvar):
        mine = jnp.where(lane // rows == v, total, 0.0)
        interp = jnp.sum(mine, axis=1, keepdims=True)
        head = out_ref[0, v, :, :LANES]
        out_ref[0, v, :, :LANES] = head - jnp.where(lane == 0, interp, 0.0)


def shards(perturbation, jacobian, flux_theta, flux_merid, donor_rows, donor_weights):
    count, far, ring = lax.axis_size(INST), lax.axis_size(FAR), lax.axis_size(RING)
    ndom = lax.axis_size(DOM)
    _, nvar, rows, cells = perturbation.shape
    smem = pl.BlockSpec(memory_space=pltpu.SMEM)
    hbm = pl.BlockSpec(memory_space=pltpu.HBM)
    blocks, face, sibling, outer = call(
        prepare,
        (perturbation,),
        whole(1),
        (
            jax.ShapeDtypeStruct((count, nvar // 2, rows, LANES), jnp.bfloat16),
            jax.ShapeDtypeStruct((ring * 2, 1, LANES), F32),
            jax.ShapeDtypeStruct((nvar, cells), F32),
            jax.ShapeDtypeStruct((nvar, cells), F32),
        ),
        10**6,
        "prepare",
    )
    swaps = [(c, (c + (1 if c % 2 else -1)) % ndom) for c in range(ndom)]
    outer = lax.ppermute(outer, DOM, swaps)
    near = lax.all_to_all(face, (RING, CORE), 0, 0, tiled=True)
    pair = lax.all_gather(sibling, CORE, axis=0)
    got = lax.all_to_all(blocks, INST, 0, 0, tiled=True)
    mixed = call(
        mix,
        (got, outer, pair),
        whole(1) + [pl.BlockSpec(memory_space=pl.ANY)] * 2,
        (jax.ShapeDtypeStruct((count, nvar // 2, rows, LANES), F32),),
        2 * 16 * nvar * rows * cells,
        "mix",
    )[0]
    near, mixed, pair = lax.optimization_barrier((near, mixed, pair))
    others = [lax.ppermute(near, FAR, [(f, (f + s) % far) for f in range(far)]) for s in range(1, far)]
    back = lax.all_to_all(mixed, INST, 0, 0, tiled=True)
    total = call(
        functools.partial(space, count),
        (perturbation, jacobian, flux_theta, flux_merid, pair, outer),
        [hbm] * 4 + whole(2),
        (jax.ShapeDtypeStruct((nvar, rows, cells), F32),),
        2 * 18 * nvar * rows * cells,
        "space",
        [
            pltpu.VMEM(perturbation.shape, F32),
            pltpu.VMEM(jacobian.shape, F32),
            pltpu.SMEM((nvar, nvar), F32),
            pltpu.SMEM((nvar, nvar), F32),
            pltpu.VMEM((nvar, rows, cells), F32),
            pltpu.SemaphoreType.DMA((4,)),
        ],
    )[0]
    return call(
        finish,
        (total, back, near) + tuple(others) + (donor_weights, donor_rows),
        whole(7) + [smem],
        (jax.ShapeDtypeStruct(perturbation.shape, F32),),
        3 * nvar * rows * cells,
        "finish",
        [pltpu.VMEM((far * ring * 2, 1, LANES), F32), pltpu.VMEM((2, rows, LANES), F32)],
    )[0]


def solution(mesh):
    inst = mesh.devices.shape[0]
    fine = Mesh(mesh.devices.reshape(inst, 8, 4, 2), (INST,) + DOM)
    in_specs = (
        P(INST, None, DOM, None),
        P(INST, None, None, DOM, None),
        P(),
        P(),
        P(INST, None, DOM),
        P(INST, None, DOM),
    )
    out_specs = P(INST, None, DOM, None)
    return jax.shard_map(shards, mesh=fine, in_specs=in_specs, out_specs=out_specs, check_vma=False)
```

```python
import functools
import math

import jax
import jax.numpy as jnp
from jax import lax
from jax.experimental import pallas as pl
from jax.experimental.pallas import tpu as pltpu
from jax.sharding import Mesh, PartitionSpec as P

OMEGA = 0.5
NYQUIST = 2.0
INST = "inst"
RING, FAR, CORE = "ring", "far", "core"
DOM = (RING, FAR, CORE)
LANES = 128
F32 = jnp.float32
VMEM_BYTES = 12 * 2**20


def whole(count):
    return [pl.BlockSpec(memory_space=pltpu.VMEM) for _ in range(count)]


def call(body, operands, specs, outs, flops, name, scratch=(), out_specs=None):
    moved = sum(math.prod(v.shape) * v.dtype.itemsize for v in list(operands) + list(outs))
    return pl.pallas_call(
        body,
        out_shape=outs,
        in_specs=specs,
        out_specs=out_specs or whole(len(outs)),
        scratch_shapes=scratch,
        compiler_params=pltpu.CompilerParams(vmem_limit_bytes=VMEM_BYTES),
        cost_estimate=pl.CostEstimate(flops=flops, bytes_accessed=moved, transcendentals=0),
        name=name,
    )(*operands)


def antisymmetric(count):
    return [OMEGA * 0.5 * (-1) ** k / math.tan(math.pi * k / count) for k in range(1, count // 2)]


def prepare(p_ref, blocks_ref, face_ref, sibling_ref, outer_ref):
    nvar, rows, cells = p_ref.shape[1:]
    chunks = cells // LANES
    upper = lax.axis_index(CORE) == 1
    low = p_ref[0].astype(jnp.bfloat16)
    third = nvar // 2
    for h in range(2):
        for c in range(chunks):
            blocks_ref[h * chunks + c] = low[h * third : (h + 1) * third, :, c * LANES : (c + 1) * LANES]
    lane = lax.broadcasted_iota(jnp.int32, (rows, LANES), 1)
    line = lax.broadcasted_iota(jnp.int32, (rows, LANES), 0)
    picked = jnp.zeros((rows, LANES), F32)
    for v in range(nvar):
        last = jnp.broadcast_to(p_ref[0, v, :, cells - 1 : cells], (rows, LANES))
        picked = jnp.where(lane == v * rows + line, last, picked)
    face = jnp.sum(picked, axis=0, keepdims=True)
    for k in range(face_ref.shape[0]):
        face_ref[k] = face
    first, final = p_ref[0, :, 0, :], p_ref[0, :, rows - 1, :]
    sibling_ref[...] = jnp.where(upper, first, final)
    outer_ref[...] = jnp.where(upper, final, first)


def mix(got_ref, outer_ref, pair_ref, mixed_ref):
    del outer_ref, pair_ref
    count, third = got_ref.shape[0], got_ref.shape[1]
    half = count // 2
    deriv = antisymmetric(count)
    for v in range(third):
        a = [got_ref[j, v].astype(F32) for j in range(count)]
        even, odd = a[0], a[1]
        for j in range(2, count, 2):
            even, odd = even + a[j], odd + a[j + 1]
        filt = (even - odd) * (NYQUIST / count)
        for i in range(half):
            gap = [a[(i - k) % count] - a[(i + k) % count] for k in range(1, half)]
            here, there = deriv[0] * gap[0], deriv[half - 2] * gap[0]
            for k in range(1, half - 1):
                here, there = here + deriv[k] * gap[k], there + deriv[half - 2 - k] * gap[k]
            sign = filt if i % 2 == 0 else -filt
            mixed_ref[i, v] = here + sign
            mixed_ref[i + half, v] = (sign if half % 2 == 0 else -sign) - there


def space(count, p_hbm, jac_hbm, theta_hbm, merid_hbm, pair_ref, outer_ref, rows_ref, weights_ref, out_ref, select_ref, within_ref, p_ref, jac_ref, theta_ref, merid_ref, dm_ref, sems):
    copies = [
        pltpu.make_async_copy(source, target, sems.at[k])
        for k, (source, target) in enumerate(
            [(p_hbm, p_ref), (theta_hbm, theta_ref), (merid_hbm, merid_ref), (jac_hbm, jac_ref)]
        )
    ]
    for copy in copies:
        copy.start()
    nvar, rows, cells = p_ref.shape[1:]
    core = lax.axis_index(CORE)
    upper = core == 1
    lane = lax.broadcasted_iota(jnp.int32, (rows, cells), 1)
    line = lax.broadcasted_iota(jnp.int32, (rows, LANES), 0)
    narrow = lax.broadcasted_iota(jnp.int32, (rows, LANES), 1)
    square = (rows, rows)
    eye = lax.broadcasted_iota(jnp.int32, square, 0) == lax.broadcasted_iota(jnp.int32, square, 1)
    places = lax.broadcasted_iota(jnp.int32, select_ref.shape[1:], 1)
    me = lax.axis_index(FAR)
    for donor in range(2):
        given = jnp.broadcast_to(rows_ref[0, donor : donor + 1, :], square)
        given = jnp.sum(jnp.where(eye, given, 0).astype(F32), axis=1, keepdims=True).astype(jnp.int32)
        weight = jnp.broadcast_to(weights_ref[0, donor : donor + 1, :], square)
        weight = jnp.sum(jnp.where(eye, weight, 0.0), axis=1, keepdims=True)
        device, spot = given >> 4, given & 15
        place = (((device >> 1) & 3) ^ me) * 16 + (device >> 3) * 2 + (device & 1)
        select_ref[donor] = jnp.where(places == place, weight, 0.0)
        within_ref[donor] = jnp.where((narrow & 15) == spot, 1.0, 0.0)
    copies[0].wait()
    for b in range(nvar):
        x = p_ref[0, b]
        right = jnp.where(lane == cells - 1, 0.0, pltpu.roll(x, cells - 1, 1))
        left = jnp.where(lane == 0, 0.0, pltpu.roll(x, 1, 1))
        dm_ref[b] = right - left
    for copy in copies[1:]:
        copy.wait()
    for c in range(cells // LANES):
        part = slice(c * LANES, (c + 1) * LANES)
        sibling = pair_ref[1 - core, :, part]
        outer = outer_ref[:, part]
        before = jnp.where(upper, sibling, outer)
        after = jnp.where(upper, outer, sibling)
        xs, ths, dms = [], [], []
        for b in range(nvar):
            x = p_ref[0, b, :, part]
            up = jnp.where(line == rows - 1, after[b : b + 1], pltpu.roll(x, rows - 1, 0))
            down = jnp.where(line == 0, before[b : b + 1], pltpu.roll(x, 1, 0))
            xs.append(x)
            ths.append(up - down)
            dms.append(dm_ref[b, :, part])
        for a in range(nvar):
            acc = (xs[a] - xs[a].astype(jnp.bfloat16).astype(F32)) * (NYQUIST / count)
            if c == 0:
                acc = acc + jnp.where(narrow == 0, xs[a], 0.0)
            for b in range(nvar):
                acc = acc + jac_ref[0, a, b, :, part] * xs[b]
                acc = acc + theta_ref[a, b] * ths[b]
                acc = acc + merid_ref[a, b] * dms[b]
            out_ref[a, :, part] = acc


def finish(sum_ref, back_ref, f0_ref, f1_ref, f2_ref, f3_ref, select_ref, within_ref, out_hbm, out_ref, faces_ref, sems):
    nvar, rows, cells = sum_ref.shape
    chunks = cells // LANES
    third = nvar // 2
    near = f0_ref.shape[0]
    for s, ref in enumerate((f0_ref, f1_ref, f2_ref, f3_ref)):
        for k in range(near):
            faces_ref[s * near + k : s * near + k + 1, :] = ref[k]
    lane = lax.broadcasted_iota(jnp.int32, (rows, LANES), 1)
    total = jnp.zeros((rows, LANES), F32)
    for donor in range(2):
        picked = jnp.dot(
            select_ref[donor], faces_ref[...], precision=lax.Precision.HIGHEST, preferred_element_type=F32
        )
        total = total + picked * within_ref[donor]
    copies = []
    for v in range(nvar):
        mine = jnp.where(lane // rows == v, total, 0.0)
        interp = jnp.sum(mine, axis=1, keepdims=True)
        for c in range(chunks):
            part = slice(c * LANES, (c + 1) * LANES)
            both = sum_ref[v, :, part] + back_ref[v // third * chunks + c, v % third]
            out_ref[v, :, part] = both - jnp.where(lane == 0, interp, 0.0) if c == 0 else both
        copies.append(pltpu.make_async_copy(out_ref.at[v], out_hbm.at[0, v], sems.at[v]))
        copies[v].start()
    for copy in copies:
        copy.wait()


def shards(perturbation, jacobian, flux_theta, flux_merid, donor_rows, donor_weights):
    count, far, ring = lax.axis_size(INST), lax.axis_size(FAR), lax.axis_size(RING)
    ndom = lax.axis_size(DOM)
    _, nvar, rows, cells = perturbation.shape
    hbm = pl.BlockSpec(memory_space=pltpu.HBM)
    blocks, face, sibling, outer = call(
        prepare,
        (perturbation,),
        whole(1),
        (
            jax.ShapeDtypeStruct((count, nvar // 2, rows, LANES), jnp.bfloat16),
            jax.ShapeDtypeStruct((ring * 2, 1, LANES), F32),
            jax.ShapeDtypeStruct((nvar, cells), F32),
            jax.ShapeDtypeStruct((nvar, cells), F32),
        ),
        10**6,
        "prepare",
    )
    swaps = [(c, (c + (1 if c % 2 else -1)) % ndom) for c in range(ndom)]
    outer = lax.ppermute(outer, DOM, swaps)
    near = lax.all_to_all(face, (RING, CORE), 0, 0, tiled=True)
    pair = lax.all_gather(sibling, CORE, axis=0)
    got = lax.all_to_all(blocks, INST, 0, 0, tiled=True)
    mixed = call(
        mix,
        (got, outer, pair),
        whole(1) + [pl.BlockSpec(memory_space=pl.ANY)] * 2,
        (jax.ShapeDtypeStruct((count, nvar // 2, rows, LANES), F32),),
        2 * 16 * nvar * rows * cells,
        "mix",
    )[0]
    near, mixed, pair = lax.optimization_barrier((near, mixed, pair))
    others = [lax.ppermute(near, FAR, [(f, f ^ s) for f in range(far)]) for s in range(1, far)]
    back = lax.all_to_all(mixed, INST, 0, 0, tiled=True)
    total, select, within = call(
        functools.partial(space, count),
        (perturbation, jacobian, flux_theta, flux_merid, pair, outer, donor_rows, donor_weights),
        [hbm] * 4 + whole(4),
        (
            jax.ShapeDtypeStruct((nvar, rows, cells), F32),
            jax.ShapeDtypeStruct((2, rows, far * ring * 2), F32),
            jax.ShapeDtypeStruct((2, rows, LANES), F32),
        ),
        2 * 18 * nvar * rows * cells,
        "space",
        [
            pltpu.VMEM(perturbation.shape, F32),
            pltpu.VMEM(jacobian.shape, F32),
            pltpu.SMEM((nvar, nvar), F32),
            pltpu.SMEM((nvar, nvar), F32),
            pltpu.VMEM((nvar, rows, cells), F32),
            pltpu.SemaphoreType.DMA((4,)),
        ],
    )
    return call(
        finish,
        (total, back, near) + tuple(others) + (select, within),
        whole(8),
        (jax.ShapeDtypeStruct(perturbation.shape, F32),),
        3 * nvar * rows * cells,
        "finish",
        [
            pltpu.VMEM((nvar, rows, cells), F32),
            pltpu.VMEM((far * ring * 2, LANES), F32),
            pltpu.SemaphoreType.DMA((nvar,)),
        ],
        [hbm],
    )[0]


def solution(mesh):
    inst = mesh.devices.shape[0]
    fine = Mesh(mesh.devices.reshape(inst, 8, 4, 2), (INST,) + DOM)
    in_specs = (
        P(INST, None, DOM, None),
        P(INST, None, None, DOM, None),
        P(),
        P(),
        P(INST, None, DOM),
        P(INST, None, DOM),
    )
    out_specs = P(INST, None, DOM, None)
    return jax.shard_map(shards, mesh=fine, in_specs=in_specs, out_specs=out_specs, check_vma=False)
```

```python
import functools
import math

import jax
import jax.numpy as jnp
from jax import lax
from jax.experimental import pallas as pl
from jax.experimental.pallas import tpu as pltpu
from jax.sharding import Mesh, PartitionSpec as P

OMEGA = 0.5
NYQUIST = 2.0
INST = "inst"
RING, FAR, CORE = "ring", "far", "core"
DOM = (RING, FAR, CORE)
LANES = 128
F32 = jnp.float32
VMEM_BYTES = 12 * 2**20


def whole(count):
    return [pl.BlockSpec(memory_space=pltpu.VMEM) for _ in range(count)]


def call(body, operands, specs, outs, flops, name, scratch=(), out_specs=None, grid=()):
    moved = sum(math.prod(v.shape) * v.dtype.itemsize for v in list(operands) + list(outs))
    return pl.pallas_call(
        body,
        grid=grid,
        out_shape=outs,
        in_specs=specs,
        out_specs=out_specs or whole(len(outs)),
        scratch_shapes=scratch,
        compiler_params=pltpu.CompilerParams(vmem_limit_bytes=VMEM_BYTES),
        cost_estimate=pl.CostEstimate(flops=flops, bytes_accessed=moved, transcendentals=0),
        name=name,
    )(*operands)


def antisymmetric(count):
    return [OMEGA * 0.5 * (-1) ** k / math.tan(math.pi * k / count) for k in range(1, count // 2)]


def prepare(p_ref, blocks_ref, face_ref, sibling_ref, outer_ref):
    third, rows, cells = p_ref.shape[1:]
    upper = lax.axis_index(CORE) == 1
    low = p_ref[0].astype(jnp.bfloat16)
    for c in range(cells // LANES):
        blocks_ref[c] = low[:, :, c * LANES : (c + 1) * LANES]
    lane = lax.broadcasted_iota(jnp.int32, (rows, LANES), 1)
    line = lax.broadcasted_iota(jnp.int32, (rows, LANES), 0)

    def rest(h):
        picked = jnp.zeros((rows, LANES), F32)
        for v in range(third):
            last = jnp.broadcast_to(p_ref[0, v, :, cells - 1 : cells], (rows, LANES))
            picked = jnp.where(lane == (h * third + v) * rows + line, last, picked)
        face = jnp.sum(picked, axis=0, keepdims=True)
        for k in range(face_ref.shape[0]):
            face_ref[k] = face if h == 0 else face_ref[k] + face
        first, final = p_ref[0, :, 0, :], p_ref[0, :, rows - 1, :]
        sibling_ref[h * third : (h + 1) * third] = jnp.where(upper, first, final)
        outer_ref[h * third : (h + 1) * third] = jnp.where(upper, final, first)

    pl.when(pl.program_id(0) == 0)(lambda: rest(0))
    pl.when(pl.program_id(0) == 1)(lambda: rest(1))


def mix(got_ref, outer_ref, pair_ref, mixed_ref):
    del outer_ref, pair_ref
    count, third = got_ref.shape[0], got_ref.shape[1]
    half = count // 2
    deriv = antisymmetric(count)
    for v in range(third):
        a = [got_ref[j, v].astype(F32) for j in range(count)]
        even, odd = a[0], a[1]
        for j in range(2, count, 2):
            even, odd = even + a[j], odd + a[j + 1]
        filt = (even - odd) * (NYQUIST / count)
        for i in range(half):
            gap = [a[(i - k) % count] - a[(i + k) % count] for k in range(1, half)]
            here, there = deriv[0] * gap[0], deriv[half - 2] * gap[0]
            for k in range(1, half - 1):
                here, there = here + deriv[k] * gap[k], there + deriv[half - 2 - k] * gap[k]
            sign = filt if i % 2 == 0 else -filt
            mixed_ref[i, v] = here + sign
            mixed_ref[i + half, v] = (sign if half % 2 == 0 else -sign) - there


def space(count, p_hbm, jac_hbm, theta_hbm, merid_hbm, pair_ref, outer_ref, rows_ref, weights_ref, out_ref, select_ref, within_ref, p_ref, jac_ref, theta_ref, merid_ref, dm_ref, sems):
    copies = [
        pltpu.make_async_copy(source, target, sems.at[k])
        for k, (source, target) in enumerate(
            [(p_hbm, p_ref), (theta_hbm, theta_ref), (merid_hbm, merid_ref), (jac_hbm, jac_ref)]
        )
    ]
    for copy in copies:
        copy.start()
    nvar, rows, cells = p_ref.shape[1:]
    core = lax.axis_index(CORE)
    upper = core == 1
    lane = lax.broadcasted_iota(jnp.int32, (rows, cells), 1)
    line = lax.broadcasted_iota(jnp.int32, (rows, LANES), 0)
    narrow = lax.broadcasted_iota(jnp.int32, (rows, LANES), 1)
    square = (rows, rows)
    eye = lax.broadcasted_iota(jnp.int32, square, 0) == lax.broadcasted_iota(jnp.int32, square, 1)
    places = lax.broadcasted_iota(jnp.int32, select_ref.shape[1:], 1)
    me = lax.axis_index(FAR)
    for donor in range(2):
        given = jnp.broadcast_to(rows_ref[0, donor : donor + 1, :], square)
        given = jnp.sum(jnp.where(eye, given, 0).astype(F32), axis=1, keepdims=True).astype(jnp.int32)
        weight = jnp.broadcast_to(weights_ref[0, donor : donor + 1, :], square)
        weight = jnp.sum(jnp.where(eye, weight, 0.0), axis=1, keepdims=True)
        device, spot = given >> 4, given & 15
        place = (((device >> 1) & 3) ^ me) * 16 + (device >> 3) * 2 + (device & 1)
        select_ref[donor] = jnp.where(places == place, weight, 0.0)
        within_ref[donor] = jnp.where((narrow & 15) == spot, 1.0, 0.0)
    copies[0].wait()
    for b in range(nvar):
        x = p_ref[0, b]
        right = jnp.where(lane == cells - 1, 0.0, pltpu.roll(x, cells - 1, 1))
        left = jnp.where(lane == 0, 0.0, pltpu.roll(x, 1, 1))
        dm_ref[b] = right - left
    for copy in copies[1:]:
        copy.wait()
    for c in range(cells // LANES):
        part = slice(c * LANES, (c + 1) * LANES)
        sibling = pair_ref[1 - core, :, part]
        outer = outer_ref[:, part]
        before = jnp.where(upper, sibling, outer)
        after = jnp.where(upper, outer, sibling)
        xs, ths, dms = [], [], []
        for b in range(nvar):
            x = p_ref[0, b, :, part]
            up = jnp.where(line == rows - 1, after[b : b + 1], pltpu.roll(x, rows - 1, 0))
            down = jnp.where(line == 0, before[b : b + 1], pltpu.roll(x, 1, 0))
            xs.append(x)
            ths.append(up - down)
            dms.append(dm_ref[b, :, part])
        for a in range(nvar):
            acc = (xs[a] - xs[a].astype(jnp.bfloat16).astype(F32)) * (NYQUIST / count)
            if c == 0:
                acc = acc + jnp.where(narrow == 0, xs[a], 0.0)
            for b in range(nvar):
                acc = acc + jac_ref[0, a, b, :, part] * xs[b]
                acc = acc + theta_ref[a, b] * ths[b]
                acc = acc + merid_ref[a, b] * dms[b]
            out_ref[a, :, part] = acc


def finish(sum_ref, back_ref, f0_ref, f1_ref, f3_ref, f2_ref, select_ref, within_ref, out_hbm, out_ref, faces_ref, sems):
    nvar, rows, cells = sum_ref.shape
    chunks = cells // LANES
    third = nvar // 2
    near = f0_ref.shape[0]
    for s, ref in enumerate((f0_ref, f1_ref, f2_ref, f3_ref)):
        for k in range(near):
            faces_ref[s * near + k : s * near + k + 1, :] = ref[k]
    lane = lax.broadcasted_iota(jnp.int32, (rows, LANES), 1)
    total = jnp.zeros((rows, LANES), F32)
    for donor in range(2):
        picked = jnp.dot(
            select_ref[donor], faces_ref[...], precision=lax.Precision.HIGHEST, preferred_element_type=F32
        )
        total = total + picked * within_ref[donor]
    copies = []
    for v in range(nvar):
        mine = jnp.where(lane // rows == v, total, 0.0)
        interp = jnp.sum(mine, axis=1, keepdims=True)
        for c in range(chunks):
            part = slice(c * LANES, (c + 1) * LANES)
            both = sum_ref[v, :, part] + back_ref[v // third * chunks + c, v % third]
            out_ref[v, :, part] = both - jnp.where(lane == 0, interp, 0.0) if c == 0 else both
        copies.append(pltpu.make_async_copy(out_ref.at[v], out_hbm.at[0, v], sems.at[v]))
        copies[v].start()
    for copy in copies:
        copy.wait()


def shards(perturbation, jacobian, flux_theta, flux_merid, donor_rows, donor_weights):
    count, far, ring = lax.axis_size(INST), lax.axis_size(FAR), lax.axis_size(RING)
    ndom = lax.axis_size(DOM)
    _, nvar, rows, cells = perturbation.shape
    hbm = pl.BlockSpec(memory_space=pltpu.HBM)
    blocks, face, sibling, outer = call(
        prepare,
        (perturbation,),
        [pl.BlockSpec((1, nvar // 2, rows, cells), lambda h: (0, h, 0, 0))],
        (
            jax.ShapeDtypeStruct((count, nvar // 2, rows, LANES), jnp.bfloat16),
            jax.ShapeDtypeStruct((ring * 2, 1, LANES), F32),
            jax.ShapeDtypeStruct((nvar, cells), F32),
            jax.ShapeDtypeStruct((nvar, cells), F32),
        ),
        10**6,
        "prepare",
        out_specs=[
            pl.BlockSpec((count // 2, nvar // 2, rows, LANES), lambda h: (h, 0, 0, 0)),
            pl.BlockSpec((ring * 2, 1, LANES), lambda h: (0, 0, 0)),
            pl.BlockSpec((nvar, cells), lambda h: (0, 0)),
            pl.BlockSpec((nvar, cells), lambda h: (0, 0)),
        ],
        grid=(2,),
    )
    swaps = [(c, (c + (1 if c % 2 else -1)) % ndom) for c in range(ndom)]
    outer = lax.ppermute(outer, DOM, swaps)
    near = lax.all_to_all(face, (RING, CORE), 0, 0, tiled=True)
    pair = lax.all_gather(sibling, CORE, axis=0)
    got = lax.all_to_all(blocks, INST, 0, 0, tiled=True)
    mixed = call(
        mix,
        (got, outer, pair),
        whole(1) + [pl.BlockSpec(memory_space=pl.ANY)] * 2,
        (jax.ShapeDtypeStruct((count, nvar // 2, rows, LANES), F32),),
        2 * 16 * nvar * rows * cells,
        "mix",
    )[0]
    near, mixed, pair = lax.optimization_barrier((near, mixed, pair))
    others = [lax.ppermute(near, FAR, [(f, f ^ s) for f in range(far)]) for s in range(1, far)]
    back = lax.all_to_all(mixed, INST, 0, 0, tiled=True)
    total, select, within = call(
        functools.partial(space, count),
        (perturbation, jacobian, flux_theta, flux_merid, pair, outer, donor_rows, donor_weights),
        [hbm] * 4 + whole(4),
        (
            jax.ShapeDtypeStruct((nvar, rows, cells), F32),
            jax.ShapeDtypeStruct((2, rows, far * ring * 2), F32),
            jax.ShapeDtypeStruct((2, rows, LANES), F32),
        ),
        2 * 18 * nvar * rows * cells,
        "space",
        [
            pltpu.VMEM(perturbation.shape, F32),
            pltpu.VMEM(jacobian.shape, F32),
            pltpu.SMEM((nvar, nvar), F32),
            pltpu.SMEM((nvar, nvar), F32),
            pltpu.VMEM((nvar, rows, cells), F32),
            pltpu.SemaphoreType.DMA((4,)),
        ],
    )
    return call(
        finish,
        (total, back, near, others[0], others[2], others[1], select, within),
        whole(8),
        (jax.ShapeDtypeStruct(perturbation.shape, F32),),
        3 * nvar * rows * cells,
        "finish",
        [
            pltpu.VMEM((nvar, rows, cells), F32),
            pltpu.VMEM((far * ring * 2, LANES), F32),
            pltpu.SemaphoreType.DMA((nvar,)),
        ],
        [hbm],
    )[0]


def solution(mesh):
    inst = mesh.devices.shape[0]
    fine = Mesh(mesh.devices.reshape(inst, 8, 4, 2), (INST,) + DOM)
    in_specs = (
        P(INST, None, DOM, None),
        P(INST, None, None, DOM, None),
        P(),
        P(),
        P(INST, None, DOM),
        P(INST, None, DOM),
    )
    out_specs = P(INST, None, DOM, None)
    return jax.shard_map(shards, mesh=fine, in_specs=in_specs, out_specs=out_specs, check_vma=False)
```
